32 devices in a mesh: space: 2 (over y), tensor: 16 (over z, x, core).
Axes of the slice: x: 2, y: 2, z: 4, core: 2. Of those that a mesh axis runs over, the one named last changes fastest.
Arguments:
- tokens: bfloat16 [784, 6144], P('space', 'tensor'), may hold values from -6 to 6
- grad_out: bfloat16 [784, 6144], P('space', 'tensor'), may hold values from -6 to 6
- w_in: bfloat16 [6144, 12288], P(None, 'tensor'), may hold values from -0.078125 to 0.078125
- w_out: bfloat16 [12288, 6144], P('tensor'), may hold values from -0.0546875 to 0.0546875
- conv_kernel: float32 [9, 12288], P(None, 'tensor'), may hold values from -2 to 2
- conv_bias: float32 [12288], P('tensor'), may hold values from -3 to 3
Outputs:
- grad_tokens: bfloat16 [784, 6144], P('space', 'tensor')
- grad_w_in: bfloat16 [6144, 12288], P('space', 'tensor')
- grad_w_out: bfloat16 [12288, 6144], P('tensor', 'space')
- grad_kernel: float32 [9, 12288], P(None, 'tensor')
- grad_bias: float32 [12288], P('tensor')
The draws below stay inside these ranges and needn't reach their ends.
All inputs are finite; a program needn't handle non-finite values.
Results may differ from the reference program's by a relative error of at most 0.014.
Values may be sent and summed in bfloat16 or wider, within the bound.
No kernel may reach another device: no remote copies, remote signals or barrier semaphores. Data moves between devices by JAX's collectives and lax.ppermute only.
A program may use at most 192 MiB of HBM per device.

```python
import jax
import jax.numpy as jnp
from jax import lax

D = 6144
FF = 12288
GW = 56
ROWS_DEV = 7
GRID_H = 14
TOKENS = 784
N_SPACE = 2
N_TENSOR = 16


def raised(entries, key, source, target, parts, factor):
    def block_of(dim):
        return (jnp.arange(entries.shape[dim]) // (entries.shape[dim] // parts)).reshape((-1,) + (1,) * (entries.ndim - 1 - dim))

    near = jax.random.permutation(key, parts)[block_of(target)]
    far = (block_of(target) + parts // 2) % parts
    return jnp.where((block_of(source) == near) | (block_of(source) == far), factor * entries, entries)


def shard_levels(stream_key, extent, cuts, least, high):
    gain = 1.0
    for dim, shards_of in cuts:
        draws = jax.random.uniform(jax.random.fold_in(jax.random.fold_in(stream_key, 6), dim), (shards_of,), jnp.float32, least / len(cuts), high / len(cuts))
        gain = gain * jnp.repeat(jnp.exp(draws), extent[dim] // shards_of).reshape((-1,) + (1,) * (len(extent) - 1 - dim))
    return gain


def normal_values(stream_key, shape, width, reach, cuts=(), held_as=jnp.bfloat16):
    entries = width * jax.random.normal(stream_key, shape, jnp.float32)
    if cuts:
        entries = entries * shard_levels(stream_key, shape, cuts, -0.22, 0.18)
    return jnp.clip(entries, -reach, reach).astype(held_as)


def bell_draw_with(rng, dims, scale, most, pieces, heavy, kind=jnp.bfloat16):
    values = scale * jax.random.normal(rng, dims, jnp.float32)
    if pieces:
        values = values * shard_levels(rng, dims, pieces, -0.22, 0.18)
    return jnp.clip(raised(values, jax.random.fold_in(rng, 3), *heavy), -most, most).astype(kind)


def setup_inputs(seed: int = 0) -> dict:
    arg_keys = jax.random.split(jax.random.key(seed), 7)
    return {
        "tokens": bell_draw_with(arg_keys[0], (TOKENS, D), 1.0, 6.0, ((0, 2), (1, 16)), (0, 1, 16, 2.0)),
        "grad_out": bell_draw_with(arg_keys[1], (TOKENS, D), 1.0, 6.0, ((0, 2), (1, 16)), (0, 1, 16, 2.0)),
        "w_in": normal_values(arg_keys[2], (D, FF), D ** -0.5, 0.078125, ((1, 16),)),
        "w_out": normal_values(arg_keys[3], (FF, D), FF ** -0.5, 0.0546875, ((0, 16),)),
        "conv_kernel": normal_values(arg_keys[4], (9, FF), 9 ** -0.5, 2.0, ((1, 16),), jnp.float32),
        "conv_bias": normal_values(arg_keys[5], (FF,), 0.5, 3.0, ((0, 16),), jnp.float32),
    }


OFFSETS = [(-1, -1), (-1, 0), (-1, 1), (0, -1), (0, 0), (0, 1), (1, -1), (1, 0), (1, 1)]


def gelu_parts(pre):
    inner = 0.7978845608 * (pre + 0.044715 * pre * pre * pre)
    tanh_val = jnp.tanh(inner)
    value = 0.5 * pre * (1.0 + tanh_val)
    slope = 0.5 * (1.0 + tanh_val) + 0.5 * pre * (1.0 - tanh_val * tanh_val) * 0.7978845608 * (1.0 + 3.0 * 0.044715 * pre * pre)
    return value, slope


def block_sum(left, right):
    block_rows = ROWS_DEV * GW
    total = None
    for index in range(N_SPACE):
        part_l = left[index * block_rows:(index + 1) * block_rows]
        part_r = right[index * block_rows:(index + 1) * block_rows]
        term = lax.dot_general(part_l, part_r, (((0,), (0,)), ((), ())), preferred_element_type=jnp.float32)
        term = lax.optimization_barrier(term.astype(jnp.bfloat16)).astype(jnp.float32)
        total = term if total is None else total + term
    return total.astype(jnp.bfloat16)


def unit_block_sum(grad_hidden, w_in):
    block_units = FF // N_TENSOR
    total = None
    for index in range(N_TENSOR):
        part_g = grad_hidden[:, index * block_units:(index + 1) * block_units]
        part_w = w_in[:, index * block_units:(index + 1) * block_units]
        term = lax.dot_general(part_g, part_w, (((1,), (1,)), ((), ())), preferred_element_type=jnp.float32)
        term = lax.optimization_barrier(term.astype(jnp.bfloat16)).astype(jnp.float32)
        total = term if total is None else total + term
    return total.astype(jnp.bfloat16)


def reference(tokens, grad_out, w_in, w_out, conv_kernel, conv_bias):
    hidden = jnp.dot(tokens, w_in, preferred_element_type=jnp.float32).astype(jnp.bfloat16)
    grid = hidden.reshape(GRID_H, GW, FF).astype(jnp.float32)
    padded = jnp.pad(grid, ((1, 1), (1, 1), (0, 0)))
    pre = jnp.zeros((GRID_H, GW, FF), jnp.float32) + conv_bias
    for index, (da, db) in enumerate(OFFSETS):
        pre = pre + conv_kernel[index] * padded[1 + da:1 + da + GRID_H, 1 + db:1 + db + GW]
    act, slope = gelu_parts(pre)
    act = act.astype(jnp.bfloat16).reshape(TOKENS, FF)
    grad_act = lax.dot_general(grad_out, w_out, (((1,), (1,)), ((), ())), preferred_element_type=jnp.float32)
    grad_pre = (grad_act.reshape(GRID_H, GW, FF) * slope).astype(jnp.bfloat16)
    grad_w_out = block_sum(act, grad_out)
    grad_f = grad_pre.astype(jnp.float32)
    kernel_rows = []
    for index, (da, db) in enumerate(OFFSETS):
        kernel_rows.append(jnp.sum(grad_f * padded[1 + da:1 + da + GRID_H, 1 + db:1 + db + GW], axis=(0, 1)))
    grad_kernel = jnp.stack(kernel_rows)
    grad_bias = jnp.sum(grad_f, axis=(0, 1))
    grad_padded = jnp.pad(grad_f, ((1, 1), (1, 1), (0, 0)))
    grad_hidden = jnp.zeros((GRID_H, GW, FF), jnp.float32)
    for index, (da, db) in enumerate(OFFSETS):
        grad_hidden = grad_hidden + conv_kernel[index] * grad_padded[1 - da:1 - da + GRID_H, 1 - db:1 - db + GW]
    grad_hidden = grad_hidden.astype(jnp.bfloat16).reshape(TOKENS, FF)
    grad_w_in = block_sum(tokens, grad_hidden)
    grad_tokens = unit_block_sum(grad_hidden, w_in)
    return (grad_tokens, grad_w_in, grad_w_out, grad_kernel, grad_bias)
```

```python
import jax
import jax.numpy as jnp
from jax import lax
from jax.experimental import pallas as pl
from jax.experimental.pallas import tpu as pltpu
from jax.sharding import PartitionSpec as P

GW = 56
NZ, NX, NC = 4, 2, 2

OFFSETS = [(-1, -1), (-1, 0), (-1, 1), (0, -1), (0, 0), (0, 1), (1, -1), (1, 0), (1, 1)]

BF = jnp.bfloat16
F32 = jnp.float32


def gelu_parts(pre):
    inner = 0.7978845608 * (pre + 0.044715 * pre * pre * pre)
    tanh_val = jnp.tanh(inner)
    value = 0.5 * pre * (1.0 + tanh_val)
    slope = 0.5 * (1.0 + tanh_val) + 0.5 * pre * (1.0 - tanh_val * tanh_val) * 0.7978845608 * (
        1.0 + 3.0 * 0.044715 * pre * pre
    )
    return (value, slope)


def padded_2(block, sides, width):
    for axis, dim in sides:
        count = lax.axis_size(axis)
        forward = [(i, i + 1) for i in range(count - 1)]
        backward = [(target, source) for source, target in forward]
        low = lax.ppermute(
            lax.slice_in_dim(block, block.shape[dim] - width, None, axis=dim), axis, forward
        )
        high = lax.ppermute(lax.slice_in_dim(block, 0, width, axis=dim), axis, backward)
        block = jnp.concatenate([low, block, high], axis=dim)
    return block


def shards_any(tokens, grad_out, w_in, w_out, conv_kernel, conv_bias):
    tok_rows = tokens.shape[0]
    grid_rows = tok_rows // GW
    ff_local = w_in.shape[1]
    full_tokens, full_grad = (
        lax.all_gather(tokens, "tensor", axis=1, tiled=True),
        lax.all_gather(grad_out, "tensor", axis=1, tiled=True),
    )
    hidden_acc = jnp.dot(full_tokens, w_in, preferred_element_type=F32)
    grad_act = lax.dot_general(full_grad, w_out, (((1,), (1,)), ((), ())), preferred_element_type=F32)
    hidden = hidden_acc.astype(BF).reshape(grid_rows, GW, ff_local)
    rimmed = padded_2(hidden, (("space", 0),), 1)
    padded = jnp.pad(rimmed, ((0, 0), (1, 1), (0, 0))).astype(F32)
    pre = jnp.zeros((grid_rows, GW, ff_local), F32) + conv_bias
    for index, (da, db) in enumerate(OFFSETS):
        pre = pre + conv_kernel[index] * padded[1 + da : 1 + da + grid_rows, 1 + db : 1 + db + GW]
    act, slope = gelu_parts(pre)
    act = act.astype(BF).reshape(tok_rows, ff_local)
    grad_pre = (grad_act.reshape(grid_rows, GW, ff_local) * slope).astype(BF)
    out_term = lax.dot_general(act, full_grad, (((0,), (0,)), ((), ())), preferred_element_type=F32)
    grad_f = grad_pre.astype(F32)
    kernel_rows = []
    for index, (da, db) in enumerate(OFFSETS):
        kernel_rows.append(
            jnp.sum(grad_f * padded[1 + da : 1 + da + grid_rows, 1 + db : 1 + db + GW], axis=(0, 1))
        )
    kernel_terms = jnp.stack(kernel_rows)
    bias_term = jnp.sum(grad_f, axis=(0, 1))
    grad_kernel, grad_bias = lax.psum((kernel_terms, bias_term), "space")
    grad_rimmed = padded_2(grad_pre, (("space", 0),), 1)
    grad_padded = jnp.pad(grad_rimmed, ((0, 0), (1, 1), (0, 0))).astype(F32)
    grad_hidden = jnp.zeros((grid_rows, GW, ff_local), F32)
    for index, (da, db) in enumerate(OFFSETS):
        grad_hidden = (
            grad_hidden
            + conv_kernel[index] * grad_padded[1 - da : 1 - da + grid_rows, 1 - db : 1 - db + GW]
        )
    grad_hidden = grad_hidden.astype(BF).reshape(tok_rows, ff_local)
    in_term = lax.dot_general(full_tokens, grad_hidden, (((0,), (0,)), ((), ())), preferred_element_type=F32)
    grad_w_in = lax.psum_scatter(in_term.astype(BF), "space", scatter_dimension=0, tiled=True)
    grad_w_out = lax.psum_scatter(out_term.astype(BF), "space", scatter_dimension=1, tiled=True)
    token_terms = lax.dot_general(grad_hidden, w_in, (((1,), (1,)), ((), ())), preferred_element_type=F32)
    grad_tokens = lax.psum_scatter(token_terms.astype(BF), "tensor", scatter_dimension=1, tiled=True)
    return (grad_tokens, grad_w_in, grad_w_out, grad_kernel, grad_bias)


def dev(z, x, c):
    return (z * NX + x) * NC + c


ALL = [(z, x, c) for z in range(NZ) for x in range(NX) for c in range(NC)]


def go_z(v, k=1):
    return lax.ppermute(v, "tensor", [(dev(z, x, c), dev((z + k) % NZ, x, c)) for z, x, c in ALL])


def go_x(v):
    return lax.ppermute(v, "tensor", [(dev(z, x, c), dev(z, 1 - x, c)) for z, x, c in ALL])


def go_c(v):
    return lax.ppermute(v, "tensor", [(dev(z, x, c), dev(z, x, 1 - c)) for z, x, c in ALL])


def go_y(v):
    return lax.ppermute(v, "space", [(0, 1), (1, 0)])


PARAMS = dict(vmem_limit_bytes=48 * 1024 * 1024)
NN = (((1,), (0,)), ((), ()))
NT = (((1,), (1,)), ((), ()))
TN = (((0,), (0,)), ((), ()))


def project(blocks, where_own, where_sib, w_own, w_sib, acc, out_dims):
    n = len(blocks)
    rows, bw = blocks[0].shape
    wide = out_dims is NN
    ff = w_own.shape[1] if wide else w_own.shape[0]
    index = jnp.stack(list(where_own) + list(where_sib)).astype(jnp.int32)

    def body(index_ref, *refs):
        bs, (wo, ws) = refs[:n], refs[n : n + 2]
        accs = refs[n + 2 : n + 4] if acc is not None else None
        oo, os = refs[-2:]
        i = pl.program_id(0)

        @pl.when(i == 0)
        def _():
            if accs is None:
                oo[...] = jnp.zeros_like(oo)
                os[...] = jnp.zeros_like(os)
            else:
                oo[...] = accs[0][...]
                os[...] = accs[1][...]

        for k in range(n):

            @pl.when(i == k)
            def _(k=k):
                b = bs[k][...]
                os[...] += lax.dot_general(b, ws[...], out_dims, preferred_element_type=F32)
                oo[...] += lax.dot_general(b, wo[...], out_dims, preferred_element_type=F32)

    whole = lambda i, r: (0, 0)
    if wide:
        w_specs = [
            pl.BlockSpec((bw, ff), lambda i, r: (r[i], 0)),
            pl.BlockSpec((bw, ff), lambda i, r: (r[n + i], 0)),
        ]
    else:
        w_specs = [
            pl.BlockSpec((ff, bw), lambda i, r: (0, r[i])),
            pl.BlockSpec((ff, bw), lambda i, r: (0, r[n + i])),
        ]
    extra = [] if acc is None else [pl.BlockSpec((rows, ff), whole)] * 2
    return pl.pallas_call(
        body,
        grid_spec=pltpu.PrefetchScalarGridSpec(
            num_scalar_prefetch=1,
            grid=(n,),
            in_specs=[pl.BlockSpec((rows, bw), whole)] * n + w_specs + extra,
            out_specs=[pl.BlockSpec((rows, ff), whole)] * 2,
        ),
        out_shape=[jax.ShapeDtypeStruct((rows, ff), F32)] * 2,
        compiler_params=pltpu.CompilerParams(**PARAMS),
        cost_estimate=pl.CostEstimate(
            flops=4 * n * rows * bw * ff, transcendentals=0, bytes_accessed=4 * n * bw * ff + 16 * rows * ff
        ),
        name="project",
    )(index, *blocks, w_own, w_sib, *(acc or ()))


def token_grads(gh_own, gh_sib, w_own, w_sib, where_own, where_sib, bw):
    n = len(where_own)
    rows, ff = gh_own.shape
    index = jnp.stack(list(where_own) + list(where_sib)).astype(jnp.int32)

    def body(index_ref, go, gs, wo, ws, *outs):
        i = pl.program_id(0)
        t = lax.dot_general(go[...], wo[...], NT, preferred_element_type=F32)
        t = t + lax.dot_general(gs[...], ws[...], NT, preferred_element_type=F32)
        for k in range(n):

            @pl.when(i == k)
            def _(k=k):
                outs[k][...] = t.astype(BF)

    whole = lambda i, r: (0, 0)
    return pl.pallas_call(
        body,
        grid_spec=pltpu.PrefetchScalarGridSpec(
            num_scalar_prefetch=1,
            grid=(n,),
            in_specs=[
                pl.BlockSpec((rows, ff), whole),
                pl.BlockSpec((rows, ff), whole),
                pl.BlockSpec((bw, ff), lambda i, r: (r[i], 0)),
                pl.BlockSpec((bw, ff), lambda i, r: (r[n + i], 0)),
            ],
            out_specs=[pl.BlockSpec((rows, bw), whole)] * n,
        ),
        out_shape=[jax.ShapeDtypeStruct((rows, bw), BF)] * n,
        compiler_params=pltpu.CompilerParams(**PARAMS),
        cost_estimate=pl.CostEstimate(
            flops=4 * n * rows * bw * ff, transcendentals=0, bytes_accessed=4 * n * bw * ff + 2 * n * rows * bw
        ),
        name="token_grads",
    )(index, gh_own, gh_sib, w_own, w_sib)


def weight_grad(core, own, sib, left, right, by_rows):
    _, n, rows, bw = own.shape
    ff = left.shape[1]

    def body(core_ref, o, s, l, r, out):
        cc = pl.program_id(1)

        def terms(src):
            if by_rows:
                t = lax.dot_general(src[0, 0], l[...], TN, preferred_element_type=F32)
                return t + lax.dot_general(src[1, 0], r[...], TN, preferred_element_type=F32)
            t = lax.dot_general(l[...], src[0, 0], TN, preferred_element_type=F32)
            return t + lax.dot_general(r[...], src[1, 0], TN, preferred_element_type=F32)

        @pl.when(cc == 0)
        def _():
            out[...] = terms(o).astype(BF)

        @pl.when(cc == 1)
        def _():
            out[...] = terms(s).astype(BF)

    place = lambda i, k, r: 2 * i + r[0] * (1 - k) + (1 - r[0]) * k
    if by_rows:
        out_spec = pl.BlockSpec((bw, ff), lambda i, k, r: (place(i, k, r), 0))
        shape = (2 * n * bw, ff)
    else:
        out_spec = pl.BlockSpec((ff, bw), lambda i, k, r: (0, place(i, k, r)))
        shape = (ff, 2 * n * bw)
    piece = pl.BlockSpec((2, 1, rows, bw), lambda i, k, r: (0, i, 0, 0))
    whole = pl.BlockSpec((rows, ff), lambda i, k, r: (0, 0))
    return pl.pallas_call(
        body,
        grid_spec=pltpu.PrefetchScalarGridSpec(
            num_scalar_prefetch=1, grid=(n, 2), in_specs=[piece, piece, whole, whole], out_specs=out_spec
        ),
        out_shape=jax.ShapeDtypeStruct(shape, BF),
        compiler_params=pltpu.CompilerParams(**PARAMS),
        cost_estimate=pl.CostEstimate(
            flops=8 * n * rows * bw * ff, transcendentals=0, bytes_accessed=12 * n * rows * bw + 4 * n * bw * ff
        ),
        name="weight_grad",
    )(core.reshape(1).astype(jnp.int32), own, sib, left, right)


def rims(block, recv, first_band):
    zero = jnp.zeros_like(recv)
    low = jnp.where(first_band, zero, recv)
    high = jnp.where(first_band, recv, zero)
    return jnp.concatenate([low, block, high], axis=0)


def shards(tokens, grad_out, w_in, w_out, conv_kernel, conv_bias):
    rows, bw = tokens.shape
    grid_rows = rows // GW
    ff = w_in.shape[1]
    s = lax.axis_index("space")
    t = lax.axis_index("tensor")
    z, x, c = t // (NX * NC), (t // NC) % NX, t % NC
    first = s == 0
    bar = lax.optimization_barrier

    send_in = lax.dynamic_index_in_dim(w_in.reshape(NZ * NX, NC, bw, ff), 1 - c, 1, keepdims=False)
    w_in_sib = go_c(send_in.reshape(NZ * NX * bw, ff))
    send_out = lax.dynamic_index_in_dim(w_out.reshape(ff, NZ * NX, NC, bw), 1 - c, 2, keepdims=False)
    w_out_sib = go_c(send_out.reshape(ff, NZ * NX * bw))

    def sib_at(zz, xx):
        return zz * NX + xx

    def own_at(zz, xx):
        return (zz * NX + xx) * NC + c

    zs = [(z - j) % NZ for j in range(NZ)]

    ta, tx = [tokens], []
    a1, x0 = go_z(tokens), go_x(tokens)
    a1, x0 = bar((a1, x0))
    a2, x1 = go_z(a1), go_x(a1)
    a2, x1 = bar((a2, x1))
    a3, x2 = go_z(a2), go_x(a2)
    a3, x2, g0 = bar((a3, x2, grad_out))
    ta, tx = [tokens, a1, a2, a3], [x0, x1, x2]
    b1, x3 = go_z(g0), go_x(a3)
    tx.append(x3)
    b1, x3, g0 = bar((b1, x3, g0))
    b2, y0 = go_z(b1), go_x(g0)
    b2, y0 = bar((b2, y0))
    b3, y1 = go_z(b2), go_x(b1)
    b3, y1 = bar((b3, y1))
    y3, y2 = go_x(b3), go_z(y1)
    ga, gx = [g0, b1, b2, b3], [y0, y1, y2, y3]

    def both(js, a, b):
        blocks = [a[j] for j in js] + [b[j] for j in js]
        own = [own_at(zs[j], x) for j in js] + [own_at(zs[j], 1 - x) for j in js]
        sib = [sib_at(zs[j], x) for j in js] + [sib_at(zs[j], 1 - x) for j in js]
        return blocks, own, sib

    part_own, part_sib = project(*both(range(NZ), ta, tx), w_in, w_in_sib, None, NN)
    hidden = (part_own + go_c(part_sib)).astype(BF).reshape(grid_rows, GW, ff)
    edge = jnp.where(first, hidden[grid_rows - 1 :], hidden[:1])
    rimmed = rims(hidden, go_y(edge), first)
    padded = jnp.pad(rimmed, ((0, 0), (1, 1), (0, 0))).astype(F32)
    pre = jnp.zeros((grid_rows, GW, ff), F32) + conv_bias
    for index, (da, db) in enumerate(OFFSETS):
        pre = pre + conv_kernel[index] * padded[1 + da : 1 + da + grid_rows, 1 + db : 1 + db + GW]
    act, slope = gelu_parts(pre)
    act = act.astype(BF).reshape(rows, ff)
    act_other = go_y(act)

    acc = project(*both((0, 1), ga, gx), w_out, w_out_sib, None, NT)
    part_own, part_sib = project(*both((2, 3), ga, gx), w_out, w_out_sib, acc, NT)
    grad_act = part_own + go_c(part_sib)
    grad_pre = (grad_act.reshape(grid_rows, GW, ff) * slope).astype(BF)
    edge = jnp.where(first, grad_pre[grid_rows - 1 :], grad_pre[:1])
    grad_rimmed = rims(grad_pre, go_y(edge), first)
    grad_padded = jnp.pad(grad_rimmed, ((0, 0), (1, 1), (0, 0))).astype(F32)
    grad_hidden = jnp.zeros((grid_rows, GW, ff), F32)
    for index, (da, db) in enumerate(OFFSETS):
        grad_hidden = (
            grad_hidden
            + conv_kernel[index] * grad_padded[1 - da : 1 - da + grid_rows, 1 - db : 1 - db + GW]
        )
    grad_hidden = grad_hidden.astype(BF).reshape(rows, ff)
    gh_sib = go_c(grad_hidden)
    gh_other = go_y(grad_hidden)

    order = [2, 1, 3, 0]
    zd = [(z + j) % NZ for j in order]
    away = token_grads(
        grad_hidden, gh_sib, w_in, w_in_sib,
        [own_at(q, 1 - x) for q in zd], [sib_at(q, 1 - x) for q in zd], bw,
    )
    came = [go_x(v) for v in away]
    home = token_grads(
        grad_hidden, gh_sib, w_in, w_in_sib,
        [own_at(q, x) for q in zd], [sib_at(q, x) for q in zd], bw,
    )
    sums = [a.astype(F32) + b.astype(F32) for a, b in zip(home, came)]
    total = sums[3]
    for k in range(3):
        total = total + go_z(sums[k].astype(BF), order[k]).astype(F32)
    grad_tokens = total.astype(BF)

    grad_f = grad_pre.astype(F32)
    terms = []
    for index, (da, db) in enumerate(OFFSETS):
        terms.append(
            jnp.sum(grad_f * padded[1 + da : 1 + da + grid_rows, 1 + db : 1 + db + GW], axis=(0, 1))
        )
    terms = jnp.stack(terms + [jnp.sum(grad_f, axis=(0, 1))])
    terms = terms + go_y(terms)
    grad_kernel, grad_bias = terms[:9], terms[9]

    def halves(a, b):
        stack = jnp.stack([v for pair in zip(a, b) for v in pair])

        def half(h):
            picks = []
            for l in range(NZ // 2):
                j = (z - (h * (NZ // 2) + l)) % NZ
                for xx in range(NX):
                    picks.append(lax.dynamic_index_in_dim(stack, j * NX + (xx ^ x), 0))
            return jnp.concatenate(picks, axis=0)

        mine = jnp.stack([half(s), go_y(half(1 - s))])
        return mine, go_c(mine)

    grad_w_out = weight_grad(c, *halves(ga, gx), act, act_other, False)
    grad_w_in = weight_grad(c, *halves(ta, tx), grad_hidden, gh_other, True)
    return (grad_tokens, grad_w_in, grad_w_out, grad_kernel, grad_bias)


def solution(mesh):
    split = mesh.shape["space"] == 2 and mesh.shape["tensor"] == NZ * NX * NC
    return jax.shard_map(
        shards if split else shards_any,
        mesh=mesh,
        in_specs=(
            P("space", "tensor"),
            P("space", "tensor"),
            P(None, "tensor"),
            P("tensor", None),
            P(None, "tensor"),
            P("tensor"),
        ),
        out_specs=(
            P("space", "tensor"),
            P("space", "tensor"),
            P("tensor", "space"),
            P(None, "tensor"),
            P("tensor"),
        ),
        check_vma=False,
    )
```

```python
import jax
import jax.numpy as jnp
from jax import lax
from jax.experimental import pallas as pl
from jax.experimental.pallas import tpu as pltpu
from jax.sharding import PartitionSpec as P

GW = 56
NZ, NX, NC = 4, 2, 2

OFFSETS = [(-1, -1), (-1, 0), (-1, 1), (0, -1), (0, 0), (0, 1), (1, -1), (1, 0), (1, 1)]

BF = jnp.bfloat16
F32 = jnp.float32


def gelu_parts(pre):
    inner = 0.7978845608 * (pre + 0.044715 * pre * pre * pre)
    tanh_val = jnp.tanh(inner)
    value = 0.5 * pre * (1.0 + tanh_val)
    slope = 0.5 * (1.0 + tanh_val) + 0.5 * pre * (1.0 - tanh_val * tanh_val) * 0.7978845608 * (
        1.0 + 3.0 * 0.044715 * pre * pre
    )
    return (value, slope)


def padded_2(block, sides, width):
    for axis, dim in sides:
        count = lax.axis_size(axis)
        forward = [(i, i + 1) for i in range(count - 1)]
        backward = [(target, source) for source, target in forward]
        low = lax.ppermute(
            lax.slice_in_dim(block, block.shape[dim] - width, None, axis=dim), axis, forward
        )
        high = lax.ppermute(lax.slice_in_dim(block, 0, width, axis=dim), axis, backward)
        block = jnp.concatenate([low, block, high], axis=dim)
    return block


def shards_any(tokens, grad_out, w_in, w_out, conv_kernel, conv_bias):
    tok_rows = tokens.shape[0]
    grid_rows = tok_rows // GW
    ff_local = w_in.shape[1]
    full_tokens, full_grad = (
        lax.all_gather(tokens, "tensor", axis=1, tiled=True),
        lax.all_gather(grad_out, "tensor", axis=1, tiled=True),
    )
    hidden_acc = jnp.dot(full_tokens, w_in, preferred_element_type=F32)
    grad_act = lax.dot_general(full_grad, w_out, (((1,), (1,)), ((), ())), preferred_element_type=F32)
    hidden = hidden_acc.astype(BF).reshape(grid_rows, GW, ff_local)
    rimmed = padded_2(hidden, (("space", 0),), 1)
    padded = jnp.pad(rimmed, ((0, 0), (1, 1), (0, 0))).astype(F32)
    pre = jnp.zeros((grid_rows, GW, ff_local), F32) + conv_bias
    for index, (da, db) in enumerate(OFFSETS):
        pre = pre + conv_kernel[index] * padded[1 + da : 1 + da + grid_rows, 1 + db : 1 + db + GW]
    act, slope = gelu_parts(pre)
    act = act.astype(BF).reshape(tok_rows, ff_local)
    grad_pre = (grad_act.reshape(grid_rows, GW, ff_local) * slope).astype(BF)
    out_term = lax.dot_general(act, full_grad, (((0,), (0,)), ((), ())), preferred_element_type=F32)
    grad_f = grad_pre.astype(F32)
    kernel_rows = []
    for index, (da, db) in enumerate(OFFSETS):
        kernel_rows.append(
            jnp.sum(grad_f * padded[1 + da : 1 + da + grid_rows, 1 + db : 1 + db + GW], axis=(0, 1))
        )
    kernel_terms = jnp.stack(kernel_rows)
    bias_term = jnp.sum(grad_f, axis=(0, 1))
    grad_kernel, grad_bias = lax.psum((kernel_terms, bias_term), "space")
    grad_rimmed = padded_2(grad_pre, (("space", 0),), 1)
    grad_padded = jnp.pad(grad_rimmed, ((0, 0), (1, 1), (0, 0))).astype(F32)
    grad_hidden = jnp.zeros((grid_rows, GW, ff_local), F32)
    for index, (da, db) in enumerate(OFFSETS):
        grad_hidden = (
            grad_hidden
            + conv_kernel[index] * grad_padded[1 - da : 1 - da + grid_rows, 1 - db : 1 - db + GW]
        )
    grad_hidden = grad_hidden.astype(BF).reshape(tok_rows, ff_local)
    in_term = lax.dot_general(full_tokens, grad_hidden, (((0,), (0,)), ((), ())), preferred_element_type=F32)
    grad_w_in = lax.psum_scatter(in_term.astype(BF), "space", scatter_dimension=0, tiled=True)
    grad_w_out = lax.psum_scatter(out_term.astype(BF), "space", scatter_dimension=1, tiled=True)
    token_terms = lax.dot_general(grad_hidden, w_in, (((1,), (1,)), ((), ())), preferred_element_type=F32)
    grad_tokens = lax.psum_scatter(token_terms.astype(BF), "tensor", scatter_dimension=1, tiled=True)
    return (grad_tokens, grad_w_in, grad_w_out, grad_kernel, grad_bias)


def dev(z, x, c):
    return (z * NX + x) * NC + c


ALL = [(z, x, c) for z in range(NZ) for x in range(NX) for c in range(NC)]


def go_z(v, k=1):
    return lax.ppermute(v, "tensor", [(dev(z, x, c), dev((z + k) % NZ, x, c)) for z, x, c in ALL])


def go_x(v):
    return lax.ppermute(v, "tensor", [(dev(z, x, c), dev(z, 1 - x, c)) for z, x, c in ALL])


def go_c(v):
    return lax.ppermute(v, "tensor", [(dev(z, x, c), dev(z, x, 1 - c)) for z, x, c in ALL])


def go_y(v):
    return lax.ppermute(v, "space", [(0, 1), (1, 0)])


PARAMS = dict(vmem_limit_bytes=48 * 1024 * 1024)
NN = (((1,), (0,)), ((), ()))
NT = (((1,), (1,)), ((), ()))
TN = (((0,), (0,)), ((), ()))


def project(core, pairs, where, w, dims, acc=None, times=None, dtype=F32):
    n = len(pairs)
    rows, bw = pairs[0][0].shape
    wide = dims is NN
    ff = w.shape[1] if wide else w.shape[0]
    index = jnp.stack([core] + list(where)).astype(jnp.int32)
    extra = [v for v in (acc, times) if v is not None]

    def body(index_ref, *refs):
        out, total = refs[-2:]
        w_ref = refs[2 * n]
        i = pl.program_id(0)
        even = index_ref[0] == 0
        for k in range(n):

            @pl.when(i == k)
            def _(k=k):
                p, q = refs[2 * k][...], refs[2 * k + 1][...]
                b = jnp.concatenate([jnp.where(even, p, q), jnp.where(even, q, p)], axis=1)
                t = lax.dot_general(b, w_ref[...], dims, preferred_element_type=F32)
                if k > 0:
                    t = t + total[...]
                elif acc is not None:
                    t = t + refs[2 * n + 1][...]
                if k < n - 1:
                    total[...] = t
                else:
                    if times is not None:
                        t = t * refs[2 * n + len(extra)][...]
                    out[...] = t.astype(dtype)

    whole = lambda i, r: (0, 0)
    if wide:
        w_spec = pl.BlockSpec((NC * bw, ff), lambda i, r: (r[1 + i], 0))
    else:
        w_spec = pl.BlockSpec((ff, NC * bw), lambda i, r: (0, r[1 + i]))
    return pl.pallas_call(
        body,
        grid_spec=pltpu.PrefetchScalarGridSpec(
            num_scalar_prefetch=1,
            grid=(n,),
            in_specs=[pl.BlockSpec((rows, bw), whole)] * (2 * n)
            + [w_spec]
            + [pl.BlockSpec((rows, ff), whole)] * len(extra),
            out_specs=pl.BlockSpec((rows, ff), whole),
            scratch_shapes=[pltpu.VMEM((rows, ff), F32)],
        ),
        out_shape=jax.ShapeDtypeStruct((rows, ff), dtype),
        compiler_params=pltpu.CompilerParams(**PARAMS),
        cost_estimate=pl.CostEstimate(
            flops=4 * n * rows * bw * ff, transcendentals=0, bytes_accessed=4 * n * bw * ff + 8 * rows * ff
        ),
        name="project",
    )(index, *[v for pair in pairs for v in pair], w, *extra)


def token_grads(gh_own, gh_sib, w_own, w_sib, where_own, where_sib, bw):
    n = len(where_own)
    rows, ff = gh_own.shape
    index = jnp.stack(list(where_own) + list(where_sib)).astype(jnp.int32)

    def body(index_ref, go, gs, wo, ws, out):
        t = lax.dot_general(go[...], wo[...], NT, preferred_element_type=F32)
        t = t + lax.dot_general(gs[...], ws[...], NT, preferred_element_type=F32)
        out[0] = t.astype(BF)

    whole = lambda i, r: (0, 0)
    return pl.pallas_call(
        body,
        grid_spec=pltpu.PrefetchScalarGridSpec(
            num_scalar_prefetch=1,
            grid=(n,),
            in_specs=[
                pl.BlockSpec((rows, ff), whole),
                pl.BlockSpec((rows, ff), whole),
                pl.BlockSpec((bw, ff), lambda i, r: (r[i], 0)),
                pl.BlockSpec((bw, ff), lambda i, r: (r[n + i], 0)),
            ],
            out_specs=pl.BlockSpec((1, rows, bw), lambda i, r: (i, 0, 0)),
        ),
        out_shape=jax.ShapeDtypeStruct((n, rows, bw), BF),
        compiler_params=pltpu.CompilerParams(**PARAMS),
        cost_estimate=pl.CostEstimate(
            flops=4 * n * rows * bw * ff, transcendentals=0, bytes_accessed=4 * n * bw * ff + 2 * n * rows * bw
        ),
        name="token_grads",
    )(index, gh_own, gh_sib, w_own, w_sib)


def pack(w, core, by_rows, bw):
    rows, cols = w.shape
    n = (rows if by_rows else cols) // (NC * bw)

    def body(core_ref, w_ref, out_ref):
        out_ref[...] = w_ref[...]

    if by_rows:
        shape, block = (n * bw, cols), (bw, cols)
        at, to = (lambda i, r: (NC * i + 1 - r[0], 0)), (lambda i, r: (i, 0))
    else:
        shape, block = (rows, n * bw), (rows, bw)
        at, to = (lambda i, r: (0, NC * i + 1 - r[0])), (lambda i, r: (0, i))
    return pl.pallas_call(
        body,
        grid_spec=pltpu.PrefetchScalarGridSpec(
            num_scalar_prefetch=1, grid=(n,), in_specs=[pl.BlockSpec(block, at)], out_specs=pl.BlockSpec(block, to)
        ),
        out_shape=jax.ShapeDtypeStruct(shape, w.dtype),
        compiler_params=pltpu.CompilerParams(**PARAMS),
        cost_estimate=pl.CostEstimate(flops=0, transcendentals=0, bytes_accessed=2 * rows * cols),
        name="pack",
    )(core.reshape(1).astype(jnp.int32), w)


def weight_grad(core, sets, left, right, by_rows, blocks, into=None):
    n = len(sets)
    rows, bw = sets[0][3][0].shape
    ff = left.shape[1]
    wide = NC * bw
    index = jnp.stack([core] + [v for q in sets for v in q[:2]]).astype(jnp.int32)
    arrays, plan = [], []
    for _, _, mine, other in sets:
        row = []
        for key, pair in mine.items():
            row.append((key, len(arrays)))
            arrays += list(pair)
        plan.append((row, len(arrays)))
        arrays += list(other)
    m = len(arrays)

    def body(index_ref, l, r, *refs):
        src = refs[:m]
        out, buf, obuf, in_sem, out_sem = refs[-5:]
        c = index_ref[0]
        spots = [pl.multiple_of(c * bw, bw), pl.multiple_of((1 - c) * bw, bw)]

        def copy(q, at, band, cc):
            return pltpu.make_async_copy(
                src[at + cc], buf.at[q % 2, band, :, pl.ds(spots[cc], bw)], in_sem.at[q % 2, band, cc]
            )

        def load(q):
            row, other = plan[q]
            for key, at in row:

                @pl.when(index_ref[2 + 2 * q] == key)
                def _(at=at):
                    for cc in range(NC):
                        copy(q, at, 0, cc).start()

            for cc in range(NC):
                copy(q, other, 1, cc).start()

        def loaded(q):
            for band in range(2):
                for cc in range(NC):
                    copy(q, plan[q][1], band, cc).wait()

        def store(q):
            place = pl.multiple_of(index_ref[1 + 2 * q] * wide, wide)
            target = out.at[pl.ds(place, wide), :] if by_rows else out.at[:, pl.ds(place, wide)]
            return pltpu.make_async_copy(obuf.at[q % 2], target, out_sem.at[q % 2])

        load(0)
        for q in range(n):
            if q + 1 < n:
                load(q + 1)
            loaded(q)
            mine, other = buf[q % 2, 0], buf[q % 2, 1]
            if by_rows:
                t = lax.dot_general(mine, l[...], TN, preferred_element_type=F32)
                t = t + lax.dot_general(other, r[...], TN, preferred_element_type=F32)
            else:
                t = lax.dot_general(l[...], mine, TN, preferred_element_type=F32)
                t = t + lax.dot_general(r[...], other, TN, preferred_element_type=F32)
            if q >= 2:
                store(q - 2).wait()
            obuf[q % 2] = t.astype(BF)
            store(q).start()
        for q in range(max(0, n - 2), n):
            store(q).wait()

    more = [] if into is None else [into]
    shape = (blocks * wide, ff) if by_rows else (ff, blocks * wide)
    anywhere = pl.BlockSpec(memory_space=pltpu.HBM)
    inside = pl.BlockSpec((rows, ff), lambda i, r: (0, 0))
    return pl.pallas_call(
        body,
        grid_spec=pltpu.PrefetchScalarGridSpec(
            num_scalar_prefetch=1,
            grid=(1,),
            in_specs=[inside, inside] + [anywhere] * (m + len(more)),
            out_specs=anywhere,
            scratch_shapes=[
                pltpu.VMEM((2, 2, rows, wide), BF),
                pltpu.VMEM((2, wide, ff) if by_rows else (2, ff, wide), BF),
                pltpu.SemaphoreType.DMA((2, 2, NC)),
                pltpu.SemaphoreType.DMA((2,)),
            ],
        ),
        out_shape=jax.ShapeDtypeStruct(shape, BF),
        input_output_aliases={3 + m: 0} if more else {},
        compiler_params=pltpu.CompilerParams(**PARAMS),
        cost_estimate=pl.CostEstimate(
            flops=4 * n * rows * wide * ff, transcendentals=0, bytes_accessed=4 * n * rows * wide + 2 * n * wide * ff
        ),
        name="weight_grad",
    )(index, left, right, *arrays, *more)


def rims(block, recv, first_band):
    zero = jnp.zeros_like(recv)
    low = jnp.where(first_band, zero, recv)
    high = jnp.where(first_band, recv, zero)
    return jnp.concatenate([low, block, high], axis=0)


def pick(j, choices):
    items = list(choices.items())
    value = items[-1][1]
    for key, array in items[:-1]:
        value = jnp.where(j == key, array, value)
    return value


def shards(tokens, grad_out, w_in, w_out, conv_kernel, conv_bias):
    rows, bw = tokens.shape
    grid_rows = rows // GW
    ff = w_in.shape[1]
    s = lax.axis_index("space")
    t = lax.axis_index("tensor")
    z, x, c = t // (NX * NC), (t // NC) % NX, t % NC
    first = s == 0
    bar = lax.optimization_barrier

    def sib_at(zz, xx):
        return zz * NX + xx

    def own_at(zz, xx):
        return (zz * NX + xx) * NC + c

    def part(w, pieces, dims, **more):
        where = [sib_at((z - j) % NZ, x if same == 0 else 1 - x) for _, _, j, same in pieces]
        return project(c, [p[:2] for p in pieces], where, w, dims, **more)

    half, low = z // (NZ // 2), z % (NZ // 2)

    def places(side):
        l1 = jnp.where(half == side, low, 1)
        z1, z2 = side * (NZ // 2) + l1, side * (NZ // 2) + 1 - l1
        return l1, (z - z1) % NZ, (z - z2) % NZ

    _, j1, j2 = places(1 - s)
    l1, k1, k2 = places(s)
    l2 = 1 - l1
    blocks = NZ // 2 * NX

    a0 = tokens
    a1, e0, a0s = go_z(a0), go_x(a0), go_c(a0)
    pack_in = pack(w_in, c, True, bw)
    a1, e0, a0s, pack_in = bar((a1, e0, a0s, pack_in))

    a2, e1, a1s, e0s, w_in_sib = go_z(a1), go_x(a1), go_c(a1), go_c(e0), go_c(pack_in)
    a2, e1, a1s, e0s, w_in_sib = bar((a2, e1, a1s, e0s, w_in_sib))

    a3, e2, a2s, e1s = go_z(a2), go_x(a2), go_c(a2), go_c(e1)
    ya1 = go_y(pick(j1, {0: a0, 1: a1, 2: a2}))
    acc = part(w_in, [(a0, a0s, 0, 0), (e0, e0s, 0, 1), (a1, a1s, 1, 0)], NN)
    a3, e2, a2s, e1s, ya1, acc, b0 = bar((a3, e2, a2s, e1s, ya1, acc, grad_out))

    b1, e3, a3s, e2s = go_z(b0), go_x(a3), go_c(a3), go_c(e2)
    ye1 = go_y(pick(j1, {0: e0, 1: e1, 2: e2}))
    b1, e3, a3s, e2s, ye1, acc, b0 = bar((b1, e3, a3s, e2s, ye1, acc, b0))

    e3s = go_c(e3)
    b2, f0, b0s = go_z(b1), go_x(b0), go_c(b0)
    ya2 = go_y(pick(j2, {1: a1, 2: a2, 3: a3}))
    hidden = part(
        w_in,
        [(a2, a2s, 2, 0), (e1, e1s, 1, 1), (a3, a3s, 3, 0), (e2, e2s, 2, 1), (e3, e3s, 3, 1)],
        NN, acc=acc, dtype=BF,
    )
    b2, f0, b0s, ya2, e3s, hidden = bar((b2, f0, b0s, ya2, e3s, hidden))

    hidden = hidden.reshape(grid_rows, GW, ff)
    b3, f1, b1s, f0s = go_z(b2), go_x(b1), go_c(b1), go_c(f0)
    edge = jnp.where(first, hidden[grid_rows - 1 :], hidden[:1]).reshape(GW * ff // bw, bw)
    sent = jnp.concatenate([pick(j2, {1: e1, 2: e2, 3: e3}), edge], axis=0)
    came = go_y(sent)
    b3, f1, b1s, f0s, came = bar((b3, f1, b1s, f0s, came))

    ye2, halo = came[:rows], came[rows:].reshape(1, GW, ff)
    f2, f3, b2s, b3s = go_z(f1), go_x(b3), go_c(b2), go_c(b3)
    yb1 = go_y(pick(j1, {0: b0, 1: b1, 2: b2}))
    acc = part(w_out, [(b0, b0s, 0, 0), (b1, b1s, 1, 0), (f0, f0s, 0, 1), (b2, b2s, 2, 0)], NT)
    f2, f3, b2s, b3s, yb1, acc, ye2, halo = bar((f2, f3, b2s, b3s, yb1, acc, ye2, halo))

    f1s, f2s, f3s, ya1s = go_c(f1), go_c(f2), go_c(f3), go_c(ya1)
    yb2 = go_y(pick(j2, {1: b1, 2: b2, 3: b3}))
    rimmed = rims(hidden, halo, first)
    padded = jnp.pad(rimmed, ((0, 0), (1, 1), (0, 0))).astype(F32)
    pre = jnp.zeros((grid_rows, GW, ff), F32) + conv_bias
    for index, (da, db) in enumerate(OFFSETS):
        pre = pre + conv_kernel[index] * padded[1 + da : 1 + da + grid_rows, 1 + db : 1 + db + GW]
    act, slope = gelu_parts(pre)
    act, slope = act.astype(BF).reshape(rows, ff), slope.reshape(rows, ff)
    grad_pre = part(
        w_out,
        [(b3, b3s, 3, 0), (f1, f1s, 1, 1), (f2, f2s, 2, 1), (f3, f3s, 3, 1)],
        NT, acc=acc, times=slope, dtype=BF,
    )
    grad_pre, yb2, f1s, f2s, f3s, ya1s, act = bar((grad_pre, yb2, f1s, f2s, f3s, ya1s, act))

    grad_pre = grad_pre.reshape(grid_rows, GW, ff)
    halo = go_y(jnp.where(first, grad_pre[grid_rows - 1 :], grad_pre[:1]))
    yf1 = go_y(pick(j1, {0: f0, 1: f1, 2: f2}))
    ya2s, ye1s = go_c(ya2), go_c(ye1)
    halo, ya2s, ye1s, act = bar((halo, ya2s, ye1s, act))

    grad_rimmed = rims(grad_pre, halo, first)
    grad_padded = jnp.pad(grad_rimmed, ((0, 0), (1, 1), (0, 0))).astype(F32)
    grad_hidden = jnp.zeros((grid_rows, GW, ff), F32)
    for index, (da, db) in enumerate(OFFSETS):
        grad_hidden = (
            grad_hidden
            + conv_kernel[index] * grad_padded[1 - da : 1 - da + grid_rows, 1 - db : 1 - db + GW]
        )
    grad_hidden = grad_hidden.astype(BF).reshape(rows, ff)
    gh_sib, ye2s = go_c(grad_hidden), go_c(ye2)
    yf2 = go_y(pick(j2, {1: f1, 2: f2, 3: f3}))
    order = [2, 1, 3, 0]
    zd = [(z + j) % NZ for j in order]

    def grads(which, xx):
        return token_grads(
            grad_hidden, gh_sib, w_in, w_in_sib,
            [own_at(zd[k], xx) for k in which], [sib_at(zd[k], xx) for k in which], bw,
        )

    away = grads((0, 1), 1 - x)
    away, gh_sib, ye2s, act, yf1, grad_hidden = bar((away, gh_sib, ye2s, act, yf1, grad_hidden))

    came, gh_other = go_x(away), go_y(grad_hidden)
    away = grads((2, 3), 1 - x)
    home = grads((0, 1, 2, 3), x)
    yb1s, yb2s = go_c(yb1), go_c(yb2)
    grad_f = grad_pre.astype(F32)
    terms = []
    for index, (da, db) in enumerate(OFFSETS):
        terms.append(
            jnp.sum(grad_f * padded[1 + da : 1 + da + grid_rows, 1 + db : 1 + db + GW], axis=(0, 1))
        )
    terms = jnp.stack(terms + [jnp.sum(grad_f, axis=(0, 1))])
    came, gh_other, yf2, away, home, yb1s, yb2s, act, terms = bar(
        (came, gh_other, yf2, away, home, yb1s, yb2s, act, terms)
    )

    add = lambda p, q: (p.astype(F32) + q.astype(F32)).astype(BF)
    act_other, yf1s = go_y(act), go_c(yf1)
    out0, out1 = go_z(add(home[0], came[0]), order[0]), go_z(add(home[1], came[1]), order[1])
    came = go_x(away)
    from_a = {0: (a0, a0s), 1: (a1, a1s), 2: (a2, a2s), 3: (a3, a3s)}
    from_e = {0: (e0, e0s), 1: (e1, e1s), 2: (e2, e2s), 3: (e3, e3s)}
    from_b = {0: (b0, b0s), 1: (b1, b1s), 2: (b2, b2s), 3: (b3, b3s)}
    from_f = {0: (f0, f0s), 1: (f1, f1s), 2: (f2, f2s), 3: (f3, f3s)}
    grad_w_in = weight_grad(
        c,
        [
            (l1 * NX + x, k1, from_a, (ya1, ya1s)),
            (l2 * NX + x, k2, from_a, (ya2, ya2s)),
            (l1 * NX + 1 - x, k1, from_e, (ye1, ye1s)),
            (l2 * NX + 1 - x, k2, from_e, (ye2, ye2s)),
        ],
        grad_hidden, gh_other, True, blocks,
    )
    out0, out1, came, act_other, yf1s, grad_w_in = bar((out0, out1, came, act_other, yf1s, grad_w_in))

    out2, yf2s, terms_other = go_z(add(home[2], came[0]), order[2]), go_c(yf2), go_y(terms)
    grad_w_out = weight_grad(
        c,
        [
            (l1 * NX + x, k1, from_b, (yb1, yb1s)),
            (l2 * NX + x, k2, from_b, (yb2, yb2s)),
            (l1 * NX + 1 - x, k1, from_f, (yf1, yf1s)),
            (l2 * NX + 1 - x, k2, from_f, (yf2, yf2s)),
        ],
        act, act_other, False, blocks,
    )
    total = home[3].astype(F32) + came[1].astype(F32) + out0.astype(F32) + out1.astype(F32) + out2.astype(F32)
    grad_tokens = total.astype(BF)

    terms = terms + terms_other
    return (grad_tokens, grad_w_in, grad_w_out, terms[:9], terms[9])


def solution(mesh):
    split = mesh.shape["space"] == 2 and mesh.shape["tensor"] == NZ * NX * NC
    return jax.shard_map(
        shards if split else shards_any,
        mesh=mesh,
        in_specs=(
            P("space", "tensor"),
            P("space", "tensor"),
            P(None, "tensor"),
            P("tensor", None),
            P(None, "tensor"),
            P("tensor"),
        ),
        out_specs=(
            P("space", "tensor"),
            P("space", "tensor"),
            P("tensor", "space"),
            P(None, "tensor"),
            P("tensor"),
        ),
        check_vma=False,
    )
```
